128 devices in a mesh: sy: 8 (over x_hi, z), sx: 16 (over y, x_lo, core).
Axes of the slice: x: 4 (x_hi: 2, x_lo: 2; x = x_hi * 2 + x_lo), y: 4, z: 4, core: 2. Of those that a mesh axis runs over, the one named last changes fastest.
Arguments:
- exposures: bfloat16 [4, 8, 512, 8192], P(None, None, 'sy', 'sx'), may hold values from -6 to 6
- psf_kernels: bfloat16 [4, 8, 21, 21], replicated, may hold values from -0.25 to 0.25
- clip_masks: int32 [4, 8, 512, 8192], P(None, None, 'sy', 'sx'), may hold values from 0 to 255
- exposure_weights: float32 [4, 8], replicated, may hold values from 0.5 to 2
- plane_offsets: int32 [3, 8, 2], replicated, may hold values from -384 to 384, as said below
- start_flux: float32 [8, 512, 8192], P(None, 'sy', 'sx'), may hold values from -6 to 6
- start_weight: float32 [8, 512, 8192], P(None, 'sy', 'sx'), may hold values from 1 to 4
Outputs:
- stacked_flux: float32 [8, 512, 8192], P(None, 'sy', 'sx')
- stacked_weight: float32 [8, 512, 8192], P(None, 'sy', 'sx')
The draws below stay inside these ranges and needn't reach their ends.
Inputs may be any that keep to these rules, and one draw needn't show every extreme that they name: `clip_masks`: bit p of an entry is 1 where plane p clips that pixel of that exposure. plane_offsets[n, p, 0] moves rows and plane_offsets[n, p, 1] moves columns; a row offset has magnitude 64 // 4 to 48, positive for p < 4 and negative otherwise; a column offset has magnitude 512 // 4 to 384, positive for even p and negative for odd p; in every draw some row offset of each sign has magnitude 3 * 16 and some column offset of each sign has magnitude 3 * 128.
All inputs are finite; a program needn't handle non-finite values.
Results may differ from the reference program's by a relative error of at most 0.0003.
Values may be sent and summed in bfloat16 or wider, within the bound.
A program may use at most 128 MiB of HBM per device.

```python
import math
import jax
import jax.numpy as jnp
from jax import lax

TY = 64
TX = 512
PLANES = 8
NIGHTS = 4
EXPS = 8
KS = 21
NY = 512
NX = 8192


def draw_plane_offsets(key, part):
    folded = jax.random.fold_in(key, 7)
    key_rows, key_cols, key_night, key_plane = jax.random.split(folded, 4)
    table_shape = (NIGHTS - 1, PLANES)
    row_sizes = jax.random.randint(key_rows, table_shape, TY // 4, 3 * TY // 4 + 1)
    col_sizes = jax.random.randint(key_cols, table_shape, TX // 4, 3 * TX // 4 + 1)
    night_pick = jax.random.randint(key_night, (), 0, NIGHTS - 1)
    plane_pick = jax.random.randint(key_plane, (), 0, PLANES // 2)
    night_ids = lax.broadcasted_iota(jnp.int32, table_shape, 0)
    plane_ids = lax.broadcasted_iota(jnp.int32, table_shape, 1)
    on_night = night_ids == night_pick
    row_peak = on_night & ((plane_ids == plane_pick) | (plane_ids == plane_pick + PLANES // 2))
    col_peak = on_night & (plane_ids // 2 == plane_pick)
    row_sizes = jnp.where(row_peak, 3 * TY // 4, row_sizes)
    col_sizes = jnp.where(col_peak, 3 * TX // 4, col_sizes)
    row_signs = jnp.where(plane_ids < PLANES // 2, 1, -1)
    col_signs = 1 - 2 * (plane_ids % 2)
    return jnp.stack([row_sizes * row_signs, col_sizes * col_signs], axis=-1).astype(jnp.int32)


def plant(entries, own_key, least, high):
    index_at = [jax.random.randint(jax.random.fold_in(own_key, axis), (), 0, length) for axis, length in enumerate(entries.shape)]
    main_axis = entries.shape.index(max(entries.shape))
    beside = index_at[:main_axis] + [(index_at[main_axis] + 1) % entries.shape[main_axis]] + index_at[main_axis + 1:]
    return entries.at[tuple(index_at)].set(least).at[tuple(beside)].set(high)


def level_of(key, dims, shards, smallest, top_value):
    def one(position, shards_of):
        heights = jax.random.uniform(jax.random.fold_in(jax.random.fold_in(key, 6), position), (shards_of,), jnp.float32, smallest / len(shards), top_value / len(shards))
        return jnp.repeat(jnp.exp(heights), dims[position] // shards_of).reshape((-1,) + (1,) * (len(dims) - position - 1))

    gain = one(*shards[0])
    for cut in shards[1:]:
        gain = gain * one(*cut)
    return gain


def scatter_about(rng, extent, spread, limit, pieces=(), held_as=jnp.bfloat16):
    loudness = level_of(rng, extent, pieces, -0.22, 0.18) if pieces else 1.0
    values = jax.random.normal(rng, extent, jnp.float32) * spread * loudness
    return jnp.minimum(jnp.maximum(values, -limit), limit).astype(held_as)


def setup_inputs(seed: int = 0) -> dict:
    seeds = jax.random.split(jax.random.key(seed), 8)
    exposures = scatter_about(seeds[0], (NIGHTS, EXPS, NY, NX), 1.0, 6.0, ((2, 8), (3, 16)))
    psf_kernels = scatter_about(seeds[1], (NIGHTS, EXPS, KS, KS), (KS * KS) ** -0.5, 0.25)
    clip_masks = plant(jax.random.randint(seeds[2], (NIGHTS, EXPS, NY, NX), 0, 2 ** PLANES), jax.random.fold_in(seeds[2], 1), 0, (2 ** PLANES) - 1).astype(jnp.int32)
    exposure_weights = jnp.clip(jnp.exp(jax.random.uniform(seeds[3], (NIGHTS, EXPS), jnp.float32, math.log(0.5), math.log(2.0))), 0.5, 2.0)
    plane_offsets = draw_plane_offsets(jax.random.fold_in(seeds[7], 71), 0)
    start_flux = scatter_about(seeds[5], (PLANES, NY, NX), 1.0, 6.0, ((1, 8), (2, 16)), jnp.float32)
    start_weight = jnp.clip(jnp.exp(math.log(4.0) - 1.3862944 * jax.random.uniform(seeds[6], (PLANES, NY, NX), jnp.float32) ** level_of(seeds[6], (PLANES, NY, NX), ((1, 8), (2, 16)), -0.2, 0.2)), 1.0, 4.0)
    return {"exposures": exposures, "psf_kernels": psf_kernels, "clip_masks": clip_masks, "exposure_weights": exposure_weights, "plane_offsets": plane_offsets, "start_flux": start_flux, "start_weight": start_weight}


band_scale = 1.5
weight_floor = 1.0

def psf_filter(image, kernel):
    image_wide = image.astype(jnp.float32)
    kernel_wide = kernel.astype(jnp.float32)
    kernel_size = kernel.shape[0]
    radius = (kernel_size - 1) // 2
    rows_full = image.shape[0] + 2 * radius
    cols_full = image.shape[1] + 2 * radius
    padded = jnp.pad(image_wide, radius)
    kernel_padded = jnp.pad(kernel_wide, ((0, rows_full - kernel_size), (0, cols_full - kernel_size)))
    product = jnp.fft.rfft2(padded) * jnp.conj(jnp.fft.rfft2(kernel_padded))
    result = jnp.fft.irfft2(product, s=(rows_full, cols_full))
    return result[:image.shape[0], :image.shape[1]]

def shift_field(field, row_offset, column_offset):
    margin_rows = 3 * TY // 4
    margin_cols = 3 * TX // 4
    padded = jnp.pad(field, ((margin_rows, margin_rows), (margin_cols, margin_cols)))
    first_row = (margin_rows - row_offset).astype(jnp.int32)
    first_col = (margin_cols - column_offset).astype(jnp.int32)
    return lax.dynamic_slice(padded, (first_row, first_col), (NY, NX))

def plane_update(flux_plane, weight_plane, power, filtered, clip_mask, weight_value):
    clip_bits = clip_mask // power % 2
    running_mean = flux_plane / jnp.maximum(weight_plane, weight_floor)
    band_half = band_scale / jnp.sqrt(weight_value)
    clipped = jnp.clip(filtered, running_mean - band_half, running_mean + band_half)
    chosen = jnp.where(clip_bits == 1, clipped, filtered)
    return (flux_plane + weight_value * chosen, weight_plane + weight_value)

def move_plane(plane_items):
    flux_plane, weight_plane, row_offset, column_offset = plane_items
    return (shift_field(flux_plane, row_offset, column_offset), shift_field(weight_plane, row_offset, column_offset))

def reference(exposures, psf_kernels, clip_masks, exposure_weights, plane_offsets, start_flux, start_weight):
    powers = 2 ** jnp.arange(PLANES, dtype=jnp.int32)
    flux_stack = start_flux
    weight_stack = start_weight
    for night_index in range(NIGHTS):
        if night_index > 0:
            offsets_now = plane_offsets[night_index - 1]
            flux_stack, weight_stack = lax.map(move_plane, (flux_stack, weight_stack, offsets_now[:, 0], offsets_now[:, 1]))

        def exposure_step(frame_index, carried):
            filtered = psf_filter(exposures[night_index, frame_index], psf_kernels[night_index, frame_index])
            weight_value = exposure_weights[night_index, frame_index]
            clip_mask = clip_masks[night_index, frame_index]

            def update_one(plane_items):
                return plane_update(plane_items[0], plane_items[1], plane_items[2], filtered, clip_mask, weight_value)
            return lax.map(update_one, (carried[0], carried[1], powers))
        flux_stack, weight_stack = lax.fori_loop(0, EXPS, exposure_step, (flux_stack, weight_stack))
    return (flux_stack, weight_stack)
```

```python
import jax
import jax.numpy as jnp
from jax import lax
from jax.experimental import pallas as pl
from jax.experimental.pallas import tpu as pltpu
from jax.sharding import PartitionSpec as P

f32, bf16, i32 = jnp.float32, jnp.bfloat16, jnp.int32
band_scale = 1.5
weight_floor = 1.0
ROWS, COLS = 64, 512
MR, MC = 48, 384
PLANES, NIGHTS, EXPS, KS, RAD = 8, 4, 8, 21, 10
NEXP = NIGHTS * EXPS
STEP = 16


def send(value, axis, steps):
    count = lax.axis_size(axis)
    first, last = max(0, -steps), min(count, count - steps)
    return lax.ppermute(value, axis, [(s, s + steps) for s in range(first, last)])


def conv_body(z, kv, wbuf, zwin):
    for b in range(KS):
        b0, ph = b // 4, b % 4
        base = jnp.broadcast_to(kv[b : b + 1, :], (ROWS, 128))
        t = pltpu.roll(base, 0, 1, stride=1, stride_axis=0)
        wbuf[ph * 64 : (ph + 1) * 64, b0 * 128 : (b0 + 1) * 128] = t.astype(bf16)
    for b0 in range(6):
        zwin[b0 * 128 : (b0 + 1) * 128, :] = pltpu.roll(z, (RAD - 4 * b0) % 640, 1)
    acc = jnp.dot(wbuf[...], zwin[...], preferred_element_type=f32)
    out = acc[0:64, 0:COLS]
    for ph in range(1, 4):
        out = out + pltpu.roll(acc[ph * 64 : (ph + 1) * 64, :], 640 - ph, 1)[:, :COLS]
    return out


def conv_kernel(z_ref, kv_ref, o_ref, wbuf, zwin):
    @pl.when(pl.program_id(0) == 0)
    def _():
        wbuf[...] = jnp.zeros_like(wbuf)

    o_ref[0] = conv_body(z_ref[0], kv_ref[0], wbuf, zwin)


def conv_call(z, kv):
    return pl.pallas_call(
        conv_kernel,
        grid=(NEXP,),
        in_specs=[
            pl.BlockSpec((1, 128, 640), lambda i: (i, 0, 0)),
            pl.BlockSpec((1, 24, 128), lambda i: (i, 0, 0)),
        ],
        out_specs=pl.BlockSpec((1, ROWS, COLS), lambda i: (i, 0, 0)),
        out_shape=jax.ShapeDtypeStruct((NEXP, ROWS, COLS), f32),
        scratch_shapes=[pltpu.VMEM((256, 768), bf16), pltpu.VMEM((768, 640), bf16)],
        name="conv",
    )(z, kv)


def update_rows(flux, weight, filt_ref, mask_ref, rows, bit, wv_ref, night):
    for e in range(EXPS):
        wv = wv_ref[night, e]
        half = wv_ref[night, EXPS + e]
        filtered = filt_ref[e, rows, :]
        mask = mask_ref[e, rows, :]
        mean = flux / jnp.maximum(weight, weight_floor)
        clipped = jnp.clip(filtered, mean - half, mean + half)
        chosen = jnp.where((mask & bit) != 0, clipped, filtered)
        flux = flux + wv * chosen
        weight = weight + wv
    return flux, weight


def pack_plane(fbuf, wbuf, peak, enc, own, exps):
    for k in (4, 2, 1):
        peak = jnp.maximum(peak, pltpu.roll(peak, k, 0))
    expo = jnp.ceil(4.0 * jnp.log2(jnp.maximum(peak, 1e-30)) + 0.01)
    gain = jnp.exp2(expo * -0.25) * 32766.0
    exps[...] = expo.astype(i32)

    def step(i, c):
        rows = pl.ds(pl.multiple_of(i * 8, 8), 8)
        q = jnp.round(fbuf[rows, :] * gain).astype(i32)
        w = (wbuf[rows, :] * enc + 0.5).astype(i32)
        own[rows, :] = (q << 16) | w
        return c

    lax.fori_loop(0, ROWS // 8, step, 0)


def night_kernel(night, *refs):
    refs = list(refs)
    wv_ref = refs.pop(0)
    off_ref = refs.pop(0)
    first, final = night == 0, night == NIGHTS - 1
    if first:
        flux_ref, weight_ref = refs.pop(0), refs.pop(0)
    else:
        s_ref, r_ref = refs.pop(0), refs.pop(0)
    filt_ref, mask_ref = refs.pop(0), refs.pop(0)
    if final:
        oflux, oweight = refs.pop(0), refs.pop(0)
    else:
        own, exps = refs.pop(0), refs.pop(0)
        fbuf, wbuf = refs.pop(0), refs.pop(0)
    p = pl.program_id(0)
    bit = jnp.left_shift(jnp.int32(1), p)
    if not first:
        cext = refs.pop(0)

        @pl.when(p % 2 == 0)
        def _():
            cext[:, :MC] = r_ref[0]
            cext[:, MC : MC + COLS] = s_ref[0]

        @pl.when(p % 2 == 1)
        def _():
            cext[:, :COLS] = s_ref[0]
            cext[:, COLS : COLS + MC] = r_ref[0]

        row_off = off_ref[night - 1, 2 * p]
        col_off = off_ref[night - 1, 2 * p + 1]
        start = jnp.where(p % 2 == 0, MC - col_off, -col_off)
        tile = pl.multiple_of((start // 128) * 128, 128)
        turn = (640 - start % 128) % 640

        def window(rows):
            return pltpu.roll(cext[rows, pl.ds(tile, 640)], turn, 1)[:, :COLS]

        own_gain = jnp.exp2(window(pl.ds(64, 8)).astype(f32) * 0.25) * (1.0 / 32766.0)
        far_gain = jnp.exp2(window(pl.ds(72, 8)).astype(f32) * 0.25) * (1.0 / 32766.0)
        own_gain = jnp.concatenate([own_gain, own_gain], axis=0)
        far_gain = jnp.concatenate([far_gain, far_gain], axis=0)
        dec = wv_ref[night, 2 * EXPS]
        lo = jnp.where(p < 4, row_off, 0)
        hi = jnp.where(p < 4, ROWS, ROWS + row_off)
        lane_row = lax.broadcasted_iota(i32, (STEP, COLS), 0)

    def step(i, peak):
        rows = pl.ds(pl.multiple_of(i * STEP, STEP), STEP)
        if first:
            flux, weight = flux_ref[0, rows, :], weight_ref[0, rows, :]
        else:
            packed = window(rows)
            y = lane_row + i * STEP
            gain = jnp.where((y >= lo) & (y < hi), own_gain, far_gain)
            flux = (packed >> 16).astype(f32) * gain
            weight = (packed & 0xFFFF).astype(f32) * dec
        flux, weight = update_rows(flux, weight, filt_ref, mask_ref, rows, bit, wv_ref, night)
        if final:
            oflux[0, rows, :] = flux
            oweight[0, rows, :] = weight
            return peak
        fbuf[rows, :] = flux
        wbuf[rows, :] = weight
        size = jnp.abs(flux)
        return jnp.maximum(peak, jnp.maximum(size[:8], size[8:]))

    peak = lax.fori_loop(0, ROWS // STEP, step, jnp.zeros((8, COLS), f32))
    if not final:
        pack_plane(fbuf, wbuf, peak, wv_ref[night, 2 * EXPS + 1], own.at[0], exps.at[0])


def night_call(night, table, offsets, state, filt, masks):
    first, final = night == 0, night == NIGHTS - 1
    plane = lambda rows, cols: pl.BlockSpec((1, rows, cols), lambda p: (p, 0, 0))
    whole = pl.BlockSpec((EXPS, ROWS, COLS), lambda p: (night, 0, 0))
    state_specs = [plane(ROWS, COLS)] * 2 if first else [plane(80, COLS), plane(80, MC)]
    if final:
        out_specs = [plane(ROWS, COLS)] * 2
        out_shape = [jax.ShapeDtypeStruct((PLANES, ROWS, COLS), f32)] * 2
        scratch = []
    else:
        out_specs = [plane(ROWS, COLS), plane(8, COLS)]
        out_shape = [
            jax.ShapeDtypeStruct((PLANES, ROWS, COLS), i32),
            jax.ShapeDtypeStruct((PLANES, 8, COLS), i32),
        ]
        scratch = [pltpu.VMEM((ROWS, COLS), f32)] * 2
    if not first:
        scratch = scratch + [pltpu.VMEM((80, 1024), i32)]
    smem = pl.BlockSpec(memory_space=pltpu.SMEM)
    return pl.pallas_call(
        lambda *refs: night_kernel(night, *refs),
        grid=(PLANES,),
        in_specs=[smem, smem] + state_specs + [whole, whole],
        out_specs=out_specs,
        out_shape=out_shape,
        scratch_shapes=scratch,
        name=f"night{night}",
    )(table, offsets, *state, filt, masks)


def row_kernel(night, off_ref, own, exps, recv, out, ext):
    p = pl.program_id(0)
    row_off = off_ref[night - 1, 2 * p]

    @pl.when(p < 4)
    def _():
        ext[:MR, :] = recv[0, :MR, :]
        ext[MR : MR + ROWS, :] = own[0]

    @pl.when(p >= 4)
    def _():
        ext[:ROWS, :] = own[0]
        ext[ROWS : ROWS + MR, :] = recv[0, :MR, :]

    start = jnp.where(p < 4, MR - row_off, -row_off)
    base = pl.multiple_of((start // 8) * 8, 8)
    out[0, :ROWS, :] = pltpu.roll(ext[pl.ds(base, ROWS + 8), :], (72 - start % 8) % 72, 0)[:ROWS]
    out[0, ROWS : ROWS + 8, :] = exps[0]
    out[0, ROWS + 8 :, :] = recv[0, MR:, :]


def row_call(night, offsets, own, exps, recv):
    plane = lambda rows: pl.BlockSpec((1, rows, COLS), lambda p: (p, 0, 0))
    return pl.pallas_call(
        lambda *refs: row_kernel(night, *refs),
        grid=(PLANES,),
        in_specs=[pl.BlockSpec(memory_space=pltpu.SMEM), plane(ROWS), plane(8), plane(MR + 8)],
        out_specs=plane(80),
        out_shape=jax.ShapeDtypeStruct((PLANES, 80, COLS), i32),
        scratch_shapes=[pltpu.VMEM((ROWS + MR + 8, COLS), i32)],
        name=f"rows{night}",
    )(offsets, own, exps, recv)


def scalar_table(exposure_weights):
    totals = 4.0 + jnp.cumsum(jnp.sum(exposure_weights, axis=1))
    top = totals * 1.0001
    enc = 65535.0 / top
    dec = jnp.concatenate([jnp.ones((1,), f32), top[:-1] / 65535.0])
    half = band_scale / jnp.sqrt(exposure_weights)
    return jnp.concatenate([exposure_weights, half, dec[:, None], enc[:, None]], axis=1)


def kernel_rows(psf_kernels):
    k = psf_kernels.astype(f32).reshape(NEXP, KS, KS).transpose(0, 2, 1)
    gap = jnp.zeros((NEXP, KS, 128 - KS), f32)
    k = jnp.concatenate([k[:, :, RAD:], gap, k[:, :, :RAD]], axis=2)
    return jnp.pad(k, ((0, 0), (0, 3), (0, 0)))


def per_device(exposures, psf_kernels, clip_masks, exposure_weights, plane_offsets, flux, weight):
    e = exposures.reshape(NEXP, ROWS, COLS)
    masks = clip_masks.reshape(NEXP, ROWS, COLS)
    table = scalar_table(exposure_weights)
    offsets = plane_offsets.reshape(NIGHTS - 1, 2 * PLANES)
    above = send(e[:, ROWS - RAD :, :], "sy", 1)
    below = send(e[:, :RAD, :], "sy", -1)
    tall = jnp.concatenate([e, below, jnp.zeros((NEXP, 44, COLS), bf16), above], axis=1)
    left = send(tall[:, :, COLS - RAD :], "sx", 1)
    right = send(tall[:, :, :RAD], "sx", -1)
    z = jnp.concatenate([tall, right, jnp.zeros((NEXP, 128, 108), bf16), left], axis=2)
    filt = conv_call(z, kernel_rows(psf_kernels))
    state = (flux, weight)
    for night in range(NIGHTS):
        if night > 0:
            own, exps = state
            down = jnp.concatenate([own[:4, ROWS - MR :, :], exps[:4]], axis=1)
            up = jnp.concatenate([own[4:, :MR, :], exps[4:]], axis=1)
            recv = jnp.concatenate([send(down, "sy", 1), send(up, "sy", -1)], axis=0)
            moved = row_call(night, offsets, own, exps, recv)
            pairs = moved.reshape(4, 2, 80, COLS)
            r = send(pairs[:, 0, :, COLS - MC :], "sx", 1)
            l = send(pairs[:, 1, :, :MC], "sx", -1)
            state = (moved, jnp.stack([r, l], axis=1).reshape(PLANES, 80, MC))
        state = night_call(night, table, offsets, state, filt, masks)
    return tuple(state)


def solution(mesh):
    return jax.shard_map(
        per_device,
        mesh=mesh,
        in_specs=(
            P(None, None, "sy", "sx"),
            P(),
            P(None, None, "sy", "sx"),
            P(),
            P(),
            P(None, "sy", "sx"),
            P(None, "sy", "sx"),
        ),
        out_specs=(P(None, "sy", "sx"), P(None, "sy", "sx")),
        check_vma=False,
    )
```

```python
import jax
import jax.numpy as jnp
from jax import lax
from jax.experimental import pallas as pl
from jax.experimental.pallas import tpu as pltpu
from jax.sharding import PartitionSpec as P

f32, bf16, i32 = jnp.float32, jnp.bfloat16, jnp.int32
band_scale = 1.5
weight_floor = 1.0
ROWS, COLS = 64, 512
MR, MC = 48, 384
PLANES, NIGHTS, EXPS, KS, RAD = 8, 4, 8, 21, 10
NEXP = NIGHTS * EXPS
STEP = 16
LAG = 2
MESH = pl.DeviceIdType.MESH


def whole_kernel(table, offs, e_hbm, kv, masks_hbm, flux_hbm, weight_hbm, oflux_hbm, oweight_hbm, *scratch):
    (z, masks, flux0, weight0, filt, taps, wins, hs, hr, fbuf, wbuf, sb, rext, cext, of, ow,
     in_sem, out_sem, rh_s, rh_r, ch_s, ch_r, row_s, row_r, col_s, col_r) = scratch
    sy, sx = lax.axis_index("sy"), lax.axis_index("sx")
    ny, nx = lax.axis_size("sy"), lax.axis_size("sx")
    has = {"up": sy > 0, "down": sy < ny - 1, "left": sx > 0, "right": sx < nx - 1}
    dev = {"up": (sy - 1, sx), "down": (sy + 1, sx), "left": (sy, sx - 1), "right": (sy, sx + 1)}
    back = {"up": "down", "down": "up", "left": "right", "right": "left"}

    def remote(src, dst, ss, rs, to):
        return pltpu.make_async_remote_copy(
            src_ref=src, dst_ref=dst, send_sem=ss, recv_sem=rs, device_id=dev[to], device_id_type=MESH
        )

    def row_halo(n, to):
        k = 0 if to == "up" else 1
        first, land = (0, 64) if to == "up" else (48, 80)
        some = pl.ds(n * EXPS, EXPS)
        return remote(z.at[some, pl.ds(first, 16)], z.at[some, pl.ds(land, 16)], rh_s.at[n, k], rh_r.at[n, k], to)

    def col_halo(n, to):
        k = 0 if to == "left" else 1
        return remote(hs.at[n, k], hr.at[n, k], ch_s.at[n, k], ch_r.at[n, k], to)

    def row_copy(n, p, to):
        first, land = (8, 0) if to == "down" else (0, 64)
        return remote(sb.at[n, p, pl.ds(first, 56)], rext.at[n, p, pl.ds(land, 56)], row_s.at[n, p], row_r.at[n, p], to)

    def col_copy(n, p, to):
        first, land = (COLS, 0) if to == "right" else (0, COLS)
        return remote(cext.at[n, p, :, pl.ds(first, MC)], cext.at[n, p, :, pl.ds(land, MC)], col_s.at[n, p], col_r.at[n, p], to)

    def go(cond, copy, to, what):
        there = has[back[to]] if what == "wait_recv" else has[to]

        @pl.when(jnp.logical_and(cond, there))
        def _():
            getattr(copy(to), what)()

    def rows_go(n, p, what):
        go(p < 4, lambda to: row_copy(n, p, to), "down", what)
        go(p >= 4, lambda to: row_copy(n, p, to), "up", what)

    def cols_go(n, p, what):
        go(p % 2 == 0, lambda to: col_copy(n, p, to), "right", what)
        go(p % 2 == 1, lambda to: col_copy(n, p, to), "left", what)

    def halo_go(kind, n, sides, what):
        for to in sides:
            go(True, lambda to: kind(n, to), to, what)

    copies = [
        pltpu.make_async_copy(e_hbm, z.at[:, pl.ds(0, ROWS)], in_sem.at[0]),
        pltpu.make_async_copy(flux_hbm, flux0, in_sem.at[1]),
        pltpu.make_async_copy(weight_hbm, weight0, in_sem.at[2]),
        pltpu.make_async_copy(masks_hbm, masks, in_sem.at[3]),
    ]
    for c in copies:
        c.start()

    def clear(n, c):
        z[n, ROWS:, :] = jnp.zeros((32, COLS), bf16)
        return c

    lax.fori_loop(0, NEXP, clear, 0)
    for n in range(NIGHTS):
        hr[n] = jnp.zeros((2, 96, 128), bf16)

    def clear_planes(p, c):
        for n in range(NIGHTS - 1):
            rext[n, p, 0:56, :] = jnp.zeros((56, COLS), i32)
            rext[n, p, 64:120, :] = jnp.zeros((56, COLS), i32)
            cext[n, p, :, 0:MC] = jnp.zeros((80, MC), i32)
            cext[n, p, :, COLS:1024] = jnp.zeros((80, 512), i32)
        return c

    lax.fori_loop(0, PLANES, clear_planes, 0)
    taps[...] = jnp.zeros_like(taps)
    wins[...] = jnp.zeros_like(wins)

    barrier = pltpu.get_barrier_semaphore()
    for to in dev:
        @pl.when(has[to])
        def _():
            pl.semaphore_signal(barrier, inc=1, device_id=dev[to], device_id_type=MESH)
    pl.semaphore_wait(barrier, sum(jnp.where(has[to], 1, 0) for to in dev))

    copies[0].wait()
    halo_go(row_halo, 0, ("up", "down"), "start")
    halo_go(row_halo, 1, ("up", "down"), "start")

    lane = lax.broadcasted_iota(i32, (96, 128), 1)

    def col_halo_send(n):
        def put(j, c):
            to_left, to_right = c
            first, last = z[n * EXPS + j, :, 0:128], z[n * EXPS + j, :, 384:512]
            here = (lane >= 10 * j) & (lane < 10 * j + 10)
            to_left = jnp.where(here, pltpu.roll(first.astype(f32), 10 * j, 1), to_left)
            to_right = jnp.where(here, pltpu.roll(last.astype(f32), (10 * j + 10) % 128, 1), to_right)
            return to_left, to_right

        zero = jnp.zeros((96, 128), f32)
        to_left, to_right = lax.fori_loop(0, EXPS, put, (zero, zero))
        hs[n, 0] = to_left.astype(bf16)
        hs[n, 1] = to_right.astype(bf16)
        halo_go(col_halo, n, ("left", "right"), "start")

    def conv(n, j):
        k = n * EXPS + j
        for b in range(KS):
            b0, ph = b // 4, b % 4
            base = jnp.broadcast_to(kv[k, b : b + 1, :], (ROWS, 128))
            t = pltpu.roll(base, 0, 1, stride=1, stride_axis=0)
            taps[ph * 64 : (ph + 1) * 64, b0 * 128 : (b0 + 1) * 128] = t.astype(bf16)
        right = pltpu.roll(hr[n, 0].astype(f32), (128 - 10 * j) % 128, 1)
        left = pltpu.roll(hr[n, 1].astype(f32), (246 - 10 * j) % 128, 1)
        edge = jnp.where(lane < 10, right, jnp.where(lane >= 118, left, 0.0)).astype(bf16)
        tile = jnp.concatenate([z[k], edge], axis=1)
        for b0 in range(6):
            w = pltpu.roll(tile, (RAD - 4 * b0) % 640, 1)
            wins[b0 * 128 : b0 * 128 + 80, :] = w[:80]
            wins[b0 * 128 + 112 : b0 * 128 + 128, :] = w[80:]
        acc = jnp.dot(taps[...], wins[...], preferred_element_type=f32)
        out = acc[0:64, 0:COLS]
        for ph in range(1, 4):
            out = out + pltpu.roll(acc[ph * 64 : (ph + 1) * 64, :], 640 - ph, 1)[:, :COLS]
        filt[k] = out

    def conv_range(n, a, b):
        def one(j, c):
            conv(n, j)
            return c

        lax.fori_loop(a, b, one, 0)

    lane_row = lax.broadcasted_iota(i32, (STEP, COLS), 0)

    def bits(amount, bit, shape):
        return (jnp.full(shape, amount, i32) & bit) != 0

    def accumulate(n, p):
        first, final = n == 0, n == NIGHTS - 1
        bit = jnp.left_shift(jnp.int32(1), p)
        if not first:
            row_off = offs[n - 1, 2 * p]
            col_off = offs[n - 1, 2 * p + 1]
            start = jnp.where(p % 2 == 0, MC - col_off, -col_off)
            turn = (640 - (start & 127)) % 640

            def window(rows):
                x = cext[n - 1, p, rows, :]
                x = jnp.where(bits(start, 256, (x.shape[0], 768)), x[:, 256:], x[:, :768])
                x = jnp.where(bits(start, 128, (x.shape[0], 640)), x[:, 128:], x[:, :640])
                return pltpu.roll(x, turn, 1)[:, :COLS]

            own_gain = jnp.exp2(window(pl.ds(64, 8)).astype(f32) * 0.25) * (1.0 / 32766.0)
            far_gain = jnp.exp2(window(pl.ds(72, 8)).astype(f32) * 0.25) * (1.0 / 32766.0)
            own_gain = jnp.concatenate([own_gain, own_gain], axis=0)
            far_gain = jnp.concatenate([far_gain, far_gain], axis=0)
            dec = table[n, 2 * EXPS]
            lo = jnp.where(p < 4, row_off, 0)
            hi = jnp.where(p < 4, ROWS, ROWS + row_off)

        def step(i, peak):
            rows = pl.ds(pl.multiple_of(i * STEP, STEP), STEP)
            if first:
                flux, weight = flux0[p, rows, :], weight0[p, rows, :]
            else:
                packed = window(rows)
                y = lane_row + i * STEP
                gain = jnp.where((y >= lo) & (y < hi), own_gain, far_gain)
                flux = (packed >> 16).astype(f32) * gain
                weight = (packed & 0xFFFF).astype(f32) * dec
            for e in range(EXPS):
                wv = table[n, e]
                half = table[n, EXPS + e]
                filtered = filt[n * EXPS + e, rows, :]
                mask = masks[n * EXPS + e, rows, :]
                mean = flux / jnp.maximum(weight, weight_floor)
                clipped = jnp.clip(filtered, mean - half, mean + half)
                chosen = jnp.where((mask & bit) != 0, clipped, filtered)
                flux = flux + wv * chosen
                weight = weight + wv
            if final:
                of[p, rows, :] = flux
                ow[p, rows, :] = weight
                return peak
            fbuf[rows, :] = flux
            wbuf[rows, :] = weight
            size = jnp.abs(flux)
            return jnp.maximum(peak, jnp.maximum(size[:8], size[8:]))

        peak = lax.fori_loop(0, ROWS // STEP, step, jnp.zeros((8, COLS), f32))
        if final:
            return
        for k in (4, 2, 1):
            peak = jnp.maximum(peak, pltpu.roll(peak, k, 0))
        expo = jnp.ceil(4.0 * jnp.log2(jnp.maximum(peak, 1e-30)) + 0.01)
        gain = jnp.exp2(expo * -0.25) * 32766.0
        enc = table[n, 2 * EXPS + 1]
        base = jnp.where(p < 4, 56, 0)

        def pack(i, c):
            rows = pl.ds(pl.multiple_of(i * 8, 8), 8)
            q = jnp.round(fbuf[rows, :] * gain).astype(i32)
            w = (wbuf[rows, :] * enc + 0.5).astype(i32)
            both = (q << 16) | w
            sb[n, p, rows, :] = both
            rext[n, p, pl.ds(pl.multiple_of(base + i * 8, 8), 8), :] = both
            return c

        lax.fori_loop(0, ROWS // 8, pack, 0)
        sb[n, p, pl.ds(pl.multiple_of(jnp.where(p < 4, 8, 48), 8), 8), :] = expo.astype(i32)
        rows_go(n, p, "start")

    def shift_rows(n, p):
        rows_go(n, p, "wait_recv")
        row_off = offs[n, 2 * p]
        start = jnp.where(p < 4, 8 + MR - row_off, -row_off)
        lanes = pl.ds(pl.multiple_of(jnp.where(p % 2 == 0, MC, 0), 128), COLS)
        x = rext[n, p]
        x = jnp.concatenate([jnp.where(bits(start, 32, (88, COLS)), x[32:], x[:88]), x[88:96]], axis=0)
        x = jnp.where(bits(start, 16, (80, COLS)), x[16:], x[:80])
        x = jnp.where(bits(start, 8, (72, COLS)), x[8:], x[:72])
        moved = pltpu.roll(x, (72 - (start & 7)) % 72, 0)[:ROWS]
        own = sb[n, p, pl.ds(pl.multiple_of(jnp.where(p < 4, 8, 48), 8), 8), :]
        far = rext[n, p, pl.ds(pl.multiple_of(jnp.where(p < 4, 0, 112), 8), 8), :]
        cext[n, p, 0:ROWS, lanes] = moved
        cext[n, p, ROWS : ROWS + 8, lanes] = own
        cext[n, p, ROWS + 8 :, lanes] = far
        cols_go(n, p, "start")

    def plane_at(i):
        return (i * 5) % PLANES

    halo_go(row_halo, 0, ("up", "down"), "wait_recv")
    col_halo_send(0)
    for n in range(2, NIGHTS):
        halo_go(row_halo, n, ("up", "down"), "start")
    halo_go(col_halo, 0, ("left", "right"), "wait_recv")
    conv_range(0, 0, EXPS)
    for c in copies[1:]:
        c.wait()
    for n in range(1, NIGHTS):
        halo_go(row_halo, n, ("up", "down"), "wait_recv")
        col_halo_send(n)

    for n in range(NIGHTS):
        if n + 1 < NIGHTS:
            def body(i, c):
                p = plane_at(i)
                if n > 0:
                    cols_go(n - 1, p, "wait_recv")
                accumulate(n, p)

                @pl.when(i >= LAG)
                def _():
                    shift_rows(n, plane_at(i - LAG))
                    conv(n + 1, i - LAG)

                return c

            halo_go(col_halo, n + 1, ("left", "right"), "wait_recv")
            lax.fori_loop(0, PLANES, body, 0)

            def tail(i, c):
                shift_rows(n, plane_at(i))
                conv(n + 1, i)
                return c

            lax.fori_loop(PLANES - LAG, PLANES, tail, 0)
        else:
            def out_copies(p):
                return (
                    pltpu.make_async_copy(of.at[p], oflux_hbm.at[p], out_sem.at[0, p]),
                    pltpu.make_async_copy(ow.at[p], oweight_hbm.at[p], out_sem.at[1, p]),
                )

            def last(i, c):
                p = plane_at(i)
                cols_go(n - 1, p, "wait_recv")
                accumulate(n, p)
                for d in out_copies(p):
                    d.start()
                return c

            lax.fori_loop(0, PLANES, last, 0)

    def finish(p, c):
        for d in out_copies(p):
            d.wait()
        for n in range(NIGHTS - 1):
            rows_go(n, p, "wait_send")
            cols_go(n, p, "wait_send")
        return c

    lax.fori_loop(0, PLANES, finish, 0)
    for n in range(NIGHTS):
        halo_go(row_halo, n, ("up", "down"), "wait_send")
        halo_go(col_halo, n, ("left", "right"), "wait_send")


def whole_call(table, offsets, e, kv, masks, flux, weight):
    anywhere = pl.BlockSpec(memory_space=pl.ANY)
    smem = pl.BlockSpec(memory_space=pltpu.SMEM)
    dma = pltpu.SemaphoreType.DMA
    n = NIGHTS - 1
    vm = pltpu.VMEM
    return pl.pallas_call(
        whole_kernel,
        in_specs=[smem, smem, anywhere, pl.BlockSpec(memory_space=pltpu.VMEM), anywhere, anywhere, anywhere],
        out_specs=[anywhere, anywhere],
        out_shape=[jax.ShapeDtypeStruct((PLANES, ROWS, COLS), f32)] * 2,
        scratch_shapes=[
            vm((NEXP, 96, COLS), bf16),
            vm((NEXP, ROWS, COLS), i32),
            vm((PLANES, ROWS, COLS), f32),
            vm((PLANES, ROWS, COLS), f32),
            vm((NEXP, ROWS, COLS), f32),
            vm((256, 768), bf16),
            vm((768, 640), bf16),
            vm((NIGHTS, 2, 96, 128), bf16),
            vm((NIGHTS, 2, 96, 128), bf16),
            vm((ROWS, COLS), f32),
            vm((ROWS, COLS), f32),
            vm((n, PLANES, ROWS, COLS), i32),
            vm((n, PLANES, 120, COLS), i32),
            vm((n, PLANES, 80, 1024), i32),
            vm((PLANES, ROWS, COLS), f32),
            vm((PLANES, ROWS, COLS), f32),
            dma((4,)), dma((2, PLANES)),
            dma((NIGHTS, 2)), dma((NIGHTS, 2)), dma((NIGHTS, 2)), dma((NIGHTS, 2)),
            dma((n, PLANES)), dma((n, PLANES)), dma((n, PLANES)), dma((n, PLANES)),
        ],
        compiler_params=pltpu.CompilerParams(collective_id=0, has_side_effects=True, vmem_limit_bytes=60 << 20),
        name="stack",
    )(table, offsets, e, kv, masks, flux, weight)


def scalar_table(exposure_weights):
    totals = 4.0 + jnp.cumsum(jnp.sum(exposure_weights, axis=1))
    top = totals * 1.0001
    enc = 65535.0 / top
    dec = jnp.concatenate([jnp.ones((1,), f32), top[:-1] / 65535.0])
    half = band_scale / jnp.sqrt(exposure_weights)
    return jnp.concatenate([exposure_weights, half, dec[:, None], enc[:, None]], axis=1)


def kernel_rows(psf_kernels):
    k = psf_kernels.astype(f32).reshape(NEXP, KS, KS).transpose(0, 2, 1)
    gap = jnp.zeros((NEXP, KS, 128 - KS), f32)
    k = jnp.concatenate([k[:, :, RAD:], gap, k[:, :, :RAD]], axis=2)
    return jnp.pad(k, ((0, 0), (0, 3), (0, 0)))


def per_device(exposures, psf_kernels, clip_masks, exposure_weights, plane_offsets, flux, weight):
    e = exposures.reshape(NEXP, ROWS, COLS)
    masks = clip_masks.reshape(NEXP, ROWS, COLS)
    table = scalar_table(exposure_weights)
    offsets = plane_offsets.reshape(NIGHTS - 1, 2 * PLANES)
    return tuple(whole_call(table, offsets, e, kernel_rows(psf_kernels), masks, flux, weight))


def solution(mesh):
    return jax.shard_map(
        per_device,
        mesh=mesh,
        in_specs=(
            P(None, None, "sy", "sx"),
            P(),
            P(None, None, "sy", "sx"),
            P(),
            P(),
            P(None, "sy", "sx"),
            P(None, "sy", "sx"),
        ),
        out_specs=(P(None, "sy", "sx"), P(None, "sy", "sx")),
        check_vma=False,
    )
```

```python
import jax
import jax.numpy as jnp
from jax import lax
from jax.experimental import pallas as pl
from jax.experimental.pallas import tpu as pltpu
from jax.sharding import PartitionSpec as P

f32, bf16, i32 = jnp.float32, jnp.bfloat16, jnp.int32
band_scale = 1.5
weight_floor = 1.0
ROWS, COLS = 64, 512
MR, MC = 48, 384
PLANES, NIGHTS, EXPS, KS, RAD = 8, 4, 8, 21, 10
NEXP = NIGHTS * EXPS
STEP = 16
LAG = 3
ORDER = (2, 7, 0, 5, 3, 6, 1, 4)
MESH = pl.DeviceIdType.MESH


def whole_kernel(gains, offs, e_hbm, kv, masks_hbm, flux_hbm, weight_hbm, oflux_hbm, oweight_hbm, *scratch):
    (z, masks, flux0, weight0, filt, taps, wins, hs, hr, fbuf, wbuf, sb, rext, cext, rl, of, ow,
     in_sem, out_sem, rh_s, rh_r, ch_s, ch_r, row_s, row_r, col_s, col_r, rl_s, rl_r) = scratch
    sy, sx = lax.axis_index("sy"), lax.axis_index("sx")
    ny, nx = lax.axis_size("sy"), lax.axis_size("sx")
    has = {"up": sy > 0, "down": sy < ny - 1, "left": sx > 0, "right": sx < nx - 1}
    dev = {"up": (sy - 1, sx), "down": (sy + 1, sx), "left": (sy, sx - 1), "right": (sy, sx + 1)}
    mid = ny // 2
    relays = ny == 8
    first_hop = {"down": (mid - 1, 0), "up": (mid, ny - 1)}
    last_hop = {"down": (0, mid), "up": (ny - 1, mid - 1)}
    back = {"up": "down", "down": "up", "left": "right", "right": "left"}

    def remote(src, dst, ss, rs, to):
        return pltpu.make_async_remote_copy(
            src_ref=src, dst_ref=dst, send_sem=ss, recv_sem=rs, device_id=dev[to], device_id_type=MESH
        )

    def row_halo(n, to):
        k = 0 if to == "up" else 1
        first, land = (0, 64) if to == "up" else (48, 80)
        some = pl.ds(n * EXPS, EXPS)
        return remote(z.at[some, pl.ds(first, 16)], z.at[some, pl.ds(land, 16)], rh_s.at[n, k], rh_r.at[n, k], to)

    def col_halo(n, to):
        k = 0 if to == "left" else 1
        return remote(hs.at[n, k], hr.at[n, k], ch_s.at[n, k], ch_r.at[n, k], to)

    def row_copy(n, p, to):
        first, land = (8, 0) if to == "down" else (0, 64)
        return remote(sb.at[n, p, pl.ds(first, 56)], rext.at[n, p, pl.ds(land, 56)], row_s.at[n, p], row_r.at[n, p], to)

    def col_copy(n, p, to):
        first, land = (COLS, 0) if to == "right" else (0, COLS)
        return remote(cext.at[n, p, :, pl.ds(first, MC)], cext.at[n, p, :, pl.ds(land, MC)], col_s.at[n, p], col_r.at[n, p], to)

    def go(cond, copy, to, what):
        there = has[back[to]] if what == "wait_recv" else has[to]

        @pl.when(jnp.logical_and(cond, there))
        def _():
            getattr(copy(to), what)()

    def remote_to(src, dst, ss, rs, row):
        return pltpu.make_async_remote_copy(
            src_ref=src, dst_ref=dst, send_sem=ss, recv_sem=rs, device_id=(row, sx), device_id_type=MESH
        )

    def relay_in(n, p, to):
        first = 8 if to == "down" else 0
        k = p % 2
        return remote_to(sb.at[n, p, pl.ds(first, 56)], rl.at[n, k], row_s.at[n, p], rl_r.at[n, k], first_hop[to][1])

    def relay_out(n, p, to):
        land = 0 if to == "down" else 64
        k = p % 2
        return remote_to(rl.at[n, k], rext.at[n, p, pl.ds(land, 56)], rl_s.at[n, k], row_r.at[n, p], last_hop[to][1])

    def rows_go(n, p, what):
        for to, mine in (("down", p < 4), ("up", p >= 4)):
            if relays and what != "wait_recv":
                around = mine & (p % 4 >= 2) & (sy == first_hop[to][0])
                go(mine & jnp.logical_not(around), lambda to: row_copy(n, p, to), to, what)

                @pl.when(around)
                def _():
                    getattr(relay_in(n, p, to), what)()
            else:
                go(mine, lambda to: row_copy(n, p, to), to, what)

    def relay(n, p, what):
        if not relays:
            return
        for to, mine in (("down", p < 4), ("up", p >= 4)):
            @pl.when(mine & (p % 4 >= 2) & (sy == last_hop[to][0]))
            def _():
                if what == "start":
                    relay_in(n, p, to).wait_recv()
                getattr(relay_out(n, p, to), what)()

    def cols_go(n, p, what):
        go(p % 2 == 0, lambda to: col_copy(n, p, to), "right", what)
        go(p % 2 == 1, lambda to: col_copy(n, p, to), "left", what)

    def halo_go(kind, n, sides, what):
        for to in sides:
            go(True, lambda to: kind(n, to), to, what)

    copies = [
        pltpu.make_async_copy(e_hbm, z.at[:, pl.ds(0, ROWS)], in_sem.at[0]),
        pltpu.make_async_copy(flux_hbm, flux0, in_sem.at[1]),
        pltpu.make_async_copy(weight_hbm, weight0, in_sem.at[2]),
        pltpu.make_async_copy(masks_hbm, masks, in_sem.at[3]),
    ]
    for c in copies:
        c.start()

    def clear_edges():
        def halo(n, c):
            @pl.when(jnp.logical_not(has["down"]))
            def _():
                z[n, 64:80, :] = jnp.zeros((16, COLS), bf16)

            @pl.when(jnp.logical_not(has["up"]))
            def _():
                z[n, 80:96, :] = jnp.zeros((16, COLS), bf16)

            return c

        @pl.when(jnp.logical_not(has["up"] & has["down"]))
        def _():
            lax.fori_loop(0, NEXP, halo, 0)

        def planes(p, c):
            for n in range(NIGHTS - 1):
                @pl.when(jnp.logical_not(has["up"]) & (p < 4))
                def _():
                    rext[n, p, 0:56, :] = jnp.zeros((56, COLS), i32)

                @pl.when(jnp.logical_not(has["down"]) & (p >= 4))
                def _():
                    rext[n, p, 64:120, :] = jnp.zeros((56, COLS), i32)

                @pl.when(jnp.logical_not(has["left"]) & (p % 2 == 0))
                def _():
                    cext[n, p, :, 0:MC] = jnp.zeros((72, MC), i32)

                @pl.when(jnp.logical_not(has["right"]) & (p % 2 == 1))
                def _():
                    cext[n, p, :, COLS : COLS + MC] = jnp.zeros((72, MC), i32)

            return c

        @pl.when(jnp.logical_not(has["up"] & has["down"] & has["left"] & has["right"]))
        def _():
            lax.fori_loop(0, PLANES, planes, 0)
            for n in range(NIGHTS):
                @pl.when(jnp.logical_not(has["right"]))
                def _():
                    hr[n, 0] = jnp.zeros((96, 128), bf16)

                @pl.when(jnp.logical_not(has["left"]))
                def _():
                    hr[n, 1] = jnp.zeros((96, 128), bf16)

    clear_edges()
    taps[...] = jnp.zeros_like(taps)
    wins[...] = jnp.zeros_like(wins)

    barrier = pltpu.get_barrier_semaphore()
    for to in dev:
        @pl.when(has[to])
        def _():
            pl.semaphore_signal(barrier, inc=1, device_id=dev[to], device_id_type=MESH)
    greeted = sum(jnp.where(has[to], 1, 0) for to in dev)
    if relays:
        for a, b in ((mid - 1, 0), (0, mid), (mid, ny - 1), (ny - 1, mid - 1)):
            for here, there in ((a, b), (b, a)):
                @pl.when(sy == here)
                def _():
                    pl.semaphore_signal(barrier, inc=1, device_id=(there, sx), device_id_type=MESH)

                greeted = greeted + jnp.where(sy == here, 1, 0)
    pl.semaphore_wait(barrier, greeted)

    copies[0].wait()
    halo_go(row_halo, 0, ("up", "down"), "start")
    halo_go(row_halo, 1, ("up", "down"), "start")

    lane = lax.broadcasted_iota(i32, (96, 128), 1)

    def col_halo_send(n):
        def put(j, c):
            to_left, to_right = c
            first, last = z[n * EXPS + j, :, 0:128], z[n * EXPS + j, :, 384:512]
            here = (lane >= 10 * j) & (lane < 10 * j + 10)
            to_left = jnp.where(here, pltpu.roll(first.astype(f32), 10 * j, 1), to_left)
            to_right = jnp.where(here, pltpu.roll(last.astype(f32), (10 * j + 10) % 128, 1), to_right)
            return to_left, to_right

        zero = jnp.zeros((96, 128), f32)
        to_left, to_right = lax.fori_loop(0, EXPS, put, (zero, zero))
        hs[n, 0] = to_left.astype(bf16)
        hs[n, 1] = to_right.astype(bf16)
        halo_go(col_halo, n, ("left", "right"), "start")

    def conv(n, j):
        k = n * EXPS + j
        for b in range(KS):
            b0, ph = b // 4, b % 4
            base = jnp.broadcast_to(kv[k, b : b + 1, :], (ROWS, 128))
            t = pltpu.roll(base, 0, 1, stride=1, stride_axis=0)
            taps[ph * 64 : (ph + 1) * 64, b0 * 128 : (b0 + 1) * 128] = t.astype(bf16)
        right = pltpu.roll(hr[n, 0].astype(f32), (128 - 10 * j) % 128, 1)
        left = pltpu.roll(hr[n, 1].astype(f32), (246 - 10 * j) % 128, 1)
        edge = jnp.where(lane < 10, right, jnp.where(lane >= 118, left, 0.0)).astype(bf16)
        tile = jnp.concatenate([z[k], edge], axis=1)
        for b0 in range(6):
            w = pltpu.roll(tile, (RAD - 4 * b0) % 640, 1)
            wins[b0 * 128 : b0 * 128 + 80, :] = w[:80]
            wins[b0 * 128 + 112 : b0 * 128 + 128, :] = w[80:]
        acc = jnp.dot(taps[...], wins[...], preferred_element_type=f32)
        out = acc[0:64, 0:COLS]
        for ph in range(1, 4):
            out = out + pltpu.roll(acc[ph * 64 : (ph + 1) * 64, :], 640 - ph, 1)[:, :COLS]
        filt[k] = out

    def conv_range(n, a, b):
        def one(j, c):
            conv(n, j)
            return c

        lax.fori_loop(a, b, one, 0)

    lane_row = lax.broadcasted_iota(i32, (STEP, COLS), 0)

    def spread(value, rows):
        return jnp.full((rows, COLS), value, f32)

    def top(n):
        total = jnp.float32(4.0)
        for m in range(n + 1):
            for e in range(EXPS):
                total = total + gains[m, e]
        return total * 1.0001

    def bits(amount, bit, shape):
        return (jnp.full(shape, amount, i32) & bit) != 0

    def accumulate(n, p):
        first, final = n == 0, n == NIGHTS - 1
        bit = jnp.left_shift(jnp.int32(1), p)
        if not first:
            row_off = offs[n - 1, p, 0]
            col_off = offs[n - 1, p, 1]
            start = jnp.where(p % 2 == 0, MC - col_off, -col_off)
            turn = (640 - (start & 127)) % 640

            def window(rows):
                x = cext[n - 1, p, rows, :]
                x = jnp.where(bits(start, 256, (x.shape[0], 768)), x[:, 256:], x[:, :768])
                x = jnp.where(bits(start, 128, (x.shape[0], 640)), x[:, 128:], x[:, :640])
                return pltpu.roll(x, turn, 1)[:, :COLS]

            both = window(pl.ds(64, 8))
            over = pltpu.roll(both, 4, 0)
            low = lax.broadcasted_iota(i32, (8, COLS), 0) < 4

            def gain_of(expo):
                gain = jnp.exp2(expo.astype(f32) * 0.25) * (1.0 / 32766.0)
                return jnp.concatenate([gain, gain], axis=0)

            own_gain = gain_of(jnp.where(low, both, over))
            far_gain = gain_of(jnp.where(low, over, both))
            dec = top(n - 1) * (1.0 / 65535.0)
            lo = jnp.where(p < 4, row_off, 0)
            hi = jnp.where(p < 4, ROWS, ROWS + row_off)

        halves = []
        for e in range(EXPS):
            half = band_scale / jnp.sqrt(jnp.full((8, 128), gains[n, e], f32))
            half = jnp.concatenate([half] * (COLS // 128), axis=1)
            halves.append(jnp.concatenate([half, half], axis=0))

        def step(i, peak):
            rows = pl.ds(pl.multiple_of(i * STEP, STEP), STEP)
            if first:
                flux, weight = flux0[p, rows, :], weight0[p, rows, :]
            else:
                packed = window(rows)
                y = lane_row + i * STEP
                gain = jnp.where((y >= lo) & (y < hi), own_gain, far_gain)
                flux = (packed >> 16).astype(f32) * gain
                weight = (packed & 0xFFFF).astype(f32) * dec
            for e in range(EXPS):
                wv = gains[n, e]
                half = halves[e]
                filtered = filt[n * EXPS + e, rows, :]
                mask = masks[n * EXPS + e, rows, :]
                mean = flux / jnp.maximum(weight, weight_floor)
                clipped = jnp.clip(filtered, mean - half, mean + half)
                chosen = jnp.where((mask & bit) != 0, clipped, filtered)
                flux = flux + wv * chosen
                weight = weight + wv
            if final:
                of[p, rows, :] = flux
                ow[p, rows, :] = weight
                return peak
            fbuf[rows, :] = flux
            wbuf[rows, :] = weight
            size = jnp.abs(flux)
            return jnp.maximum(peak, jnp.maximum(size[:8], size[8:]))

        peak = lax.fori_loop(0, ROWS // STEP, step, jnp.zeros((8, COLS), f32))
        if final:
            return
        for k in (4, 2, 1):
            peak = jnp.maximum(peak, pltpu.roll(peak, k, 0))
        expo = jnp.ceil(4.0 * jnp.log2(jnp.maximum(peak, 1e-30)) + 0.01)
        gain = jnp.exp2(expo * -0.25) * 32766.0
        enc = 65535.0 / jnp.full((8, COLS), top(n), f32)
        base = jnp.where(p < 4, 56, 0)

        def pack(i, c):
            rows = pl.ds(pl.multiple_of(i * 8, 8), 8)
            q = jnp.round(fbuf[rows, :] * gain).astype(i32)
            w = (wbuf[rows, :] * enc + 0.5).astype(i32)
            both = (q << 16) | w
            sb[n, p, rows, :] = both
            rext[n, p, pl.ds(pl.multiple_of(base + i * 8, 8), 8), :] = both
            return c

        lax.fori_loop(0, ROWS // 8, pack, 0)
        sb[n, p, pl.ds(pl.multiple_of(jnp.where(p < 4, 8, 48), 8), 8), :] = expo.astype(i32)
        rows_go(n, p, "start")

    def shift_rows(n, p):
        rows_go(n, p, "wait_recv")
        row_off = offs[n, p, 0]
        start = jnp.where(p < 4, 8 + MR - row_off, -row_off)
        lanes = pl.ds(pl.multiple_of(jnp.where(p % 2 == 0, MC, 0), 128), COLS)
        x = rext[n, p]
        x = jnp.concatenate([jnp.where(bits(start, 32, (88, COLS)), x[32:], x[:88]), x[88:96]], axis=0)
        x = jnp.where(bits(start, 16, (80, COLS)), x[16:], x[:80])
        x = jnp.where(bits(start, 8, (72, COLS)), x[8:], x[:72])
        moved = pltpu.roll(x, (72 - (start & 7)) % 72, 0)[:ROWS]
        own = sb[n, p, pl.ds(pl.multiple_of(jnp.where(p < 4, 8, 48), 8), 8), :]
        far = rext[n, p, pl.ds(pl.multiple_of(jnp.where(p < 4, 0, 112), 8), 8), :]
        cext[n, p, 0:ROWS, lanes] = moved
        cext[n, p, ROWS:, lanes] = jnp.where(lax.broadcasted_iota(i32, (8, COLS), 0) < 4, own, far)
        cols_go(n, p, "start")

    def plane_at(i):
        p = ORDER[0]
        for k in range(1, PLANES):
            p = jnp.where(i == k, ORDER[k], p)
        return p

    halo_go(row_halo, 0, ("up", "down"), "wait_recv")
    col_halo_send(0)
    for n in range(2, NIGHTS):
        halo_go(row_halo, n, ("up", "down"), "start")
    halo_go(col_halo, 0, ("left", "right"), "wait_recv")
    conv_range(0, 0, EXPS)
    for c in copies[1:]:
        c.wait()
    for n in range(1, NIGHTS):
        halo_go(row_halo, n, ("up", "down"), "wait_recv")
        col_halo_send(n)

    for n in range(NIGHTS):
        if n + 1 < NIGHTS:
            def body(i, c):
                p = plane_at(i)
                if n > 0:
                    cols_go(n - 1, p, "wait_recv")
                accumulate(n, p)

                @pl.when(i >= 1)
                def _():
                    relay(n, plane_at(i - 1), "start")

                @pl.when(i >= LAG)
                def _():
                    shift_rows(n, plane_at(i - LAG))
                    conv(n + 1, i - LAG)

                return c

            halo_go(col_halo, n + 1, ("left", "right"), "wait_recv")
            lax.fori_loop(0, PLANES, body, 0)

            relay(n, jnp.int32(ORDER[-1]), "start")

            def tail(i, c):
                shift_rows(n, plane_at(i))
                conv(n + 1, i)
                return c

            lax.fori_loop(PLANES - LAG, PLANES, tail, 0)
        else:
            def out_copies(p):
                return (
                    pltpu.make_async_copy(of.at[p], oflux_hbm.at[p], out_sem.at[0, p]),
                    pltpu.make_async_copy(ow.at[p], oweight_hbm.at[p], out_sem.at[1, p]),
                )

            def last(i, c):
                p = plane_at(i)
                cols_go(n - 1, p, "wait_recv")
                accumulate(n, p)
                for d in out_copies(p):
                    d.start()
                return c

            lax.fori_loop(0, PLANES, last, 0)

    def finish(p, c):
        for d in out_copies(p):
            d.wait()
        for n in range(NIGHTS - 1):
            rows_go(n, p, "wait_send")
            cols_go(n, p, "wait_send")
            relay(n, p, "wait_send")
        return c

    lax.fori_loop(0, PLANES, finish, 0)
    for n in range(NIGHTS):
        halo_go(row_halo, n, ("up", "down"), "wait_send")
        halo_go(col_halo, n, ("left", "right"), "wait_send")


def whole_call(gains, offsets, e, kv, masks, flux, weight):
    anywhere = pl.BlockSpec(memory_space=pl.ANY)
    smem = pl.BlockSpec(memory_space=pltpu.SMEM)
    dma = pltpu.SemaphoreType.DMA
    n = NIGHTS - 1
    vm = pltpu.VMEM
    return pl.pallas_call(
        whole_kernel,
        in_specs=[smem, smem, anywhere, pl.BlockSpec(memory_space=pltpu.VMEM), anywhere, anywhere, anywhere],
        out_specs=[anywhere, anywhere],
        out_shape=[jax.ShapeDtypeStruct((PLANES, ROWS, COLS), f32)] * 2,
        scratch_shapes=[
            vm((NEXP, 96, COLS), bf16),
            vm((NEXP, ROWS, COLS), i32),
            vm((PLANES, ROWS, COLS), f32),
            vm((PLANES, ROWS, COLS), f32),
            vm((NEXP, ROWS, COLS), f32),
            vm((256, 768), bf16),
            vm((768, 640), bf16),
            vm((NIGHTS, 2, 96, 128), bf16),
            vm((NIGHTS, 2, 96, 128), bf16),
            vm((ROWS, COLS), f32),
            vm((ROWS, COLS), f32),
            vm((n, PLANES, ROWS, COLS), i32),
            vm((n, PLANES, 120, COLS), i32),
            vm((n, PLANES, 72, 1024), i32),
            vm((n, 2, 56, COLS), i32),
            vm((PLANES, ROWS, COLS), f32),
            vm((PLANES, ROWS, COLS), f32),
            dma((4,)), dma((2, PLANES)),
            dma((NIGHTS, 2)), dma((NIGHTS, 2)), dma((NIGHTS, 2)), dma((NIGHTS, 2)),
            dma((n, PLANES)), dma((n, PLANES)), dma((n, PLANES)), dma((n, PLANES)), dma((n, 2)), dma((n, 2)),
        ],
        compiler_params=pltpu.CompilerParams(collective_id=0, has_side_effects=True, vmem_limit_bytes=60 << 20),
        name="stack",
    )(gains, offsets, e, kv, masks, flux, weight)


def kernel_rows(psf_kernels):
    lane = lax.broadcasted_iota(i32, (KS, 128), 1)
    tap = lax.broadcasted_iota(i32, (KS, 128), 0)
    place = ((lane + RAD) % 128 == tap).astype(bf16)
    k = jnp.einsum("neab,al->nebl", psf_kernels, place, preferred_element_type=f32)
    return k.reshape(NEXP, KS, 128)


def per_device(exposures, psf_kernels, clip_masks, exposure_weights, plane_offsets, flux, weight):
    e = exposures.reshape(NEXP, ROWS, COLS)
    masks = clip_masks.reshape(NEXP, ROWS, COLS)
    return tuple(whole_call(exposure_weights, plane_offsets, e, kernel_rows(psf_kernels), masks, flux, weight))


def solution(mesh):
    return jax.shard_map(
        per_device,
        mesh=mesh,
        in_specs=(
            P(None, None, "sy", "sx"),
            P(),
            P(None, None, "sy", "sx"),
            P(),
            P(),
            P(None, "sy", "sx"),
            P(None, "sy", "sx"),
        ),
        out_specs=(P(None, "sy", "sx"), P(None, "sy", "sx")),
        check_vma=False,
    )
```

```python
import jax
import jax.numpy as jnp
from jax import lax
from jax.experimental import pallas as pl
from jax.experimental.pallas import tpu as pltpu
from jax.sharding import PartitionSpec as P

f32, bf16, i32 = jnp.float32, jnp.bfloat16, jnp.int32
band_scale = 1.5
weight_floor = 1.0
ROWS, COLS = 64, 512
MR, MC = 48, 384
PLANES, NIGHTS, EXPS, KS, RAD = 8, 4, 8, 21, 10
NEXP = NIGHTS * EXPS
STEP = 16
LAG = 6
ORDER = (2, 7, 0, 5, 3, 6, 1, 4)
MESH = pl.DeviceIdType.MESH


def whole_kernel(gains, offs, e_hbm, kv, masks_hbm, flux_hbm, weight_hbm, oflux_hbm, oweight_hbm, *scratch):
    (z, masks, flux0, weight0, filt, taps, wins, hs, hr, fbuf, wbuf, sb, rext, cext, rl, of, ow,
     in_sem, out_sem, rh_s, rh_r, ch_s, ch_r, row_s, row_r, col_s, col_r, rl_s, rl_r) = scratch
    sy, sx = lax.axis_index("sy"), lax.axis_index("sx")
    ny, nx = lax.axis_size("sy"), lax.axis_size("sx")
    has = {"up": sy > 0, "down": sy < ny - 1, "left": sx > 0, "right": sx < nx - 1}
    dev = {"up": (sy - 1, sx), "down": (sy + 1, sx), "left": (sy, sx - 1), "right": (sy, sx + 1)}
    mid = ny // 2
    relays = False
    first_hop = {"down": (mid - 1, 0), "up": (mid, ny - 1)}
    last_hop = {"down": (0, mid), "up": (ny - 1, mid - 1)}
    back = {"up": "down", "down": "up", "left": "right", "right": "left"}

    def remote(src, dst, ss, rs, to):
        return pltpu.make_async_remote_copy(
            src_ref=src, dst_ref=dst, send_sem=ss, recv_sem=rs, device_id=dev[to], device_id_type=MESH
        )

    def row_halo(n, to):
        k = 0 if to == "up" else 1
        first, land = (0, 64) if to == "up" else (48, 80)
        some = pl.ds(n * EXPS, EXPS)
        return remote(z.at[some, pl.ds(first, 16)], z.at[some, pl.ds(land, 16)], rh_s.at[n, k], rh_r.at[n, k], to)

    def col_halo(n, to):
        k = 0 if to == "left" else 1
        return remote(hs.at[n, k], hr.at[n, k], ch_s.at[n, k], ch_r.at[n, k], to)

    def row_copy(n, p, to):
        first, land = (8, 0) if to == "down" else (0, 64)
        return remote(sb.at[n, p, pl.ds(first, 56)], rext.at[n, p, pl.ds(land, 56)], row_s.at[n, p], row_r.at[n, p], to)

    def col_copy(n, p, to):
        first, land = (COLS, 0) if to == "right" else (0, COLS)
        return remote(cext.at[n, p, :, pl.ds(first, MC)], cext.at[n, p, :, pl.ds(land, MC)], col_s.at[n, p], col_r.at[n, p], to)

    def go(cond, copy, to, what):
        there = has[back[to]] if what == "wait_recv" else has[to]

        @pl.when(jnp.logical_and(cond, there))
        def _():
            getattr(copy(to), what)()

    def remote_to(src, dst, ss, rs, row):
        return pltpu.make_async_remote_copy(
            src_ref=src, dst_ref=dst, send_sem=ss, recv_sem=rs, device_id=(row, sx), device_id_type=MESH
        )

    def relay_in(n, p, to):
        first = 8 if to == "down" else 0
        k = p % 2
        return remote_to(sb.at[n, p, pl.ds(first, 56)], rl.at[n, k], row_s.at[n, p], rl_r.at[n, k], first_hop[to][1])

    def relay_out(n, p, to):
        land = 0 if to == "down" else 64
        k = p % 2
        return remote_to(rl.at[n, k], rext.at[n, p, pl.ds(land, 56)], rl_s.at[n, k], row_r.at[n, p], last_hop[to][1])

    def rows_go(n, p, what):
        for to, mine in (("down", p < 4), ("up", p >= 4)):
            if relays and what != "wait_recv":
                around = mine & (p % 4 >= 2) & (sy == first_hop[to][0])
                go(mine & jnp.logical_not(around), lambda to: row_copy(n, p, to), to, what)

                @pl.when(around)
                def _():
                    getattr(relay_in(n, p, to), what)()
            else:
                go(mine, lambda to: row_copy(n, p, to), to, what)

    def relay(n, p, what):
        if not relays:
            return
        for to, mine in (("down", p < 4), ("up", p >= 4)):
            @pl.when(mine & (p % 4 >= 2) & (sy == last_hop[to][0]))
            def _():
                if what == "start":
                    relay_in(n, p, to).wait_recv()
                getattr(relay_out(n, p, to), what)()

    def cols_go(n, p, what):
        go(p % 2 == 0, lambda to: col_copy(n, p, to), "right", what)
        go(p % 2 == 1, lambda to: col_copy(n, p, to), "left", what)

    def halo_go(kind, n, sides, what):
        for to in sides:
            go(True, lambda to: kind(n, to), to, what)

    copies = [
        pltpu.make_async_copy(e_hbm, z.at[:, pl.ds(0, ROWS)], in_sem.at[0]),
        pltpu.make_async_copy(flux_hbm, flux0, in_sem.at[1]),
        pltpu.make_async_copy(weight_hbm, weight0, in_sem.at[2]),
        pltpu.make_async_copy(masks_hbm, masks, in_sem.at[3]),
    ]
    for c in copies:
        c.start()

    def clear_edges():
        def halo(n, c):
            @pl.when(jnp.logical_not(has["down"]))
            def _():
                z[n, 64:80, :] = jnp.zeros((16, COLS), bf16)

            @pl.when(jnp.logical_not(has["up"]))
            def _():
                z[n, 80:96, :] = jnp.zeros((16, COLS), bf16)

            return c

        @pl.when(jnp.logical_not(has["up"] & has["down"]))
        def _():
            lax.fori_loop(0, NEXP, halo, 0)

        def planes(p, c):
            for n in range(NIGHTS - 1):
                @pl.when(jnp.logical_not(has["up"]) & (p < 4))
                def _():
                    rext[n, p, 0:56, :] = jnp.zeros((56, COLS), i32)

                @pl.when(jnp.logical_not(has["down"]) & (p >= 4))
                def _():
                    rext[n, p, 64:120, :] = jnp.zeros((56, COLS), i32)

                @pl.when(jnp.logical_not(has["left"]) & (p % 2 == 0))
                def _():
                    cext[n, p, :, 0:MC] = jnp.zeros((72, MC), i32)

                @pl.when(jnp.logical_not(has["right"]) & (p % 2 == 1))
                def _():
                    cext[n, p, :, COLS : COLS + MC] = jnp.zeros((72, MC), i32)

            return c

        @pl.when(jnp.logical_not(has["up"] & has["down"] & has["left"] & has["right"]))
        def _():
            lax.fori_loop(0, PLANES, planes, 0)
            for n in range(NIGHTS):
                @pl.when(jnp.logical_not(has["right"]))
                def _():
                    hr[n, 0] = jnp.zeros((96, 128), bf16)

                @pl.when(jnp.logical_not(has["left"]))
                def _():
                    hr[n, 1] = jnp.zeros((96, 128), bf16)

    clear_edges()
    taps[...] = jnp.zeros_like(taps)
    wins[...] = jnp.zeros_like(wins)

    barrier = pltpu.get_barrier_semaphore()
    for to in dev:
        @pl.when(has[to])
        def _():
            pl.semaphore_signal(barrier, inc=1, device_id=dev[to], device_id_type=MESH)
    greeted = sum(jnp.where(has[to], 1, 0) for to in dev)
    if relays:
        for a, b in ((mid - 1, 0), (0, mid), (mid, ny - 1), (ny - 1, mid - 1)):
            for here, there in ((a, b), (b, a)):
                @pl.when(sy == here)
                def _():
                    pl.semaphore_signal(barrier, inc=1, device_id=(there, sx), device_id_type=MESH)

                greeted = greeted + jnp.where(sy == here, 1, 0)
    pl.semaphore_wait(barrier, greeted)

    copies[0].wait()
    halo_go(row_halo, 0, ("up", "down"), "start")
    halo_go(row_halo, 1, ("up", "down"), "start")

    lane = lax.broadcasted_iota(i32, (96, 128), 1)

    def col_halo_send(n):
        def put(j, c):
            to_left, to_right = c
            first, last = z[n * EXPS + j, :, 0:128], z[n * EXPS + j, :, 384:512]
            here = (lane >= 10 * j) & (lane < 10 * j + 10)
            to_left = jnp.where(here, pltpu.roll(first.astype(f32), 10 * j, 1), to_left)
            to_right = jnp.where(here, pltpu.roll(last.astype(f32), (10 * j + 10) % 128, 1), to_right)
            return to_left, to_right

        zero = jnp.zeros((96, 128), f32)
        to_left, to_right = lax.fori_loop(0, EXPS, put, (zero, zero))
        hs[n, 0] = to_left.astype(bf16)
        hs[n, 1] = to_right.astype(bf16)
        halo_go(col_halo, n, ("left", "right"), "start")

    def conv(n, j):
        k = n * EXPS + j
        for b in range(KS):
            b0, ph = b // 4, b % 4
            base = jnp.broadcast_to(kv[k, b : b + 1, :], (ROWS, 128))
            t = pltpu.roll(base, 0, 1, stride=1, stride_axis=0)
            taps[ph * 64 : (ph + 1) * 64, b0 * 128 : (b0 + 1) * 128] = t.astype(bf16)
        right = pltpu.roll(hr[n, 0].astype(f32), (128 - 10 * j) % 128, 1)
        left = pltpu.roll(hr[n, 1].astype(f32), (246 - 10 * j) % 128, 1)
        edge = jnp.where(lane < 10, right, jnp.where(lane >= 118, left, 0.0)).astype(bf16)
        tile = jnp.concatenate([z[k], edge], axis=1)
        for b0 in range(6):
            w = pltpu.roll(tile, (RAD - 4 * b0) % 640, 1)
            wins[b0 * 128 : b0 * 128 + 80, :] = w[:80]
            wins[b0 * 128 + 112 : b0 * 128 + 128, :] = w[80:]
        acc = jnp.dot(taps[...], wins[...], preferred_element_type=f32)
        out = acc[0:64, 0:COLS]
        for ph in range(1, 4):
            out = out + pltpu.roll(acc[ph * 64 : (ph + 1) * 64, :], 640 - ph, 1)[:, :COLS]
        filt[k] = out

    def conv_range(n, a, b):
        def one(j, c):
            conv(n, j)
            return c

        lax.fori_loop(a, b, one, 0)

    lane_row = lax.broadcasted_iota(i32, (STEP, COLS), 0)

    def spread(value, rows):
        return jnp.full((rows, COLS), value, f32)

    def top(n):
        total = jnp.float32(4.0)
        for m in range(n + 1):
            for e in range(EXPS):
                total = total + gains[m, e]
        return total * 1.0001

    def bits(amount, bit, shape):
        return (jnp.full(shape, amount, i32) & bit) != 0

    def accumulate(n, p):
        first, final = n == 0, n == NIGHTS - 1
        bit = jnp.left_shift(jnp.int32(1), p)
        if not first:
            row_off = offs[n - 1, p, 0]
            col_off = offs[n - 1, p, 1]
            start = jnp.where(p % 2 == 0, MC - col_off, -col_off)
            turn = (640 - (start & 127)) % 640

            def window(rows):
                x = cext[n - 1, p, rows, :]
                x = jnp.where(bits(start, 256, (x.shape[0], 768)), x[:, 256:], x[:, :768])
                x = jnp.where(bits(start, 128, (x.shape[0], 640)), x[:, 128:], x[:, :640])
                return pltpu.roll(x, turn, 1)[:, :COLS]

            both = window(pl.ds(64, 8))
            over = pltpu.roll(both, 4, 0)
            low = lax.broadcasted_iota(i32, (8, COLS), 0) < 4

            def gain_of(expo):
                gain = jnp.exp2(expo.astype(f32) * 0.25) * (1.0 / 32766.0)
                return jnp.concatenate([gain, gain], axis=0)

            own_gain = gain_of(jnp.where(low, both, over))
            far_gain = gain_of(jnp.where(low, over, both))
            dec = top(n - 1) * (1.0 / 65535.0)
            lo = jnp.where(p < 4, row_off, 0)
            hi = jnp.where(p < 4, ROWS, ROWS + row_off)

        halves = []
        for e in range(EXPS):
            half = band_scale / jnp.sqrt(jnp.full((8, 128), gains[n, e], f32))
            half = jnp.concatenate([half] * (COLS // 128), axis=1)
            halves.append(jnp.concatenate([half, half], axis=0))

        def step(i, peak):
            rows = pl.ds(pl.multiple_of(i * STEP, STEP), STEP)
            if first:
                flux, weight = flux0[p, rows, :], weight0[p, rows, :]
            else:
                packed = window(rows)
                y = lane_row + i * STEP
                gain = jnp.where((y >= lo) & (y < hi), own_gain, far_gain)
                flux = (packed >> 16).astype(f32) * gain
                weight = (packed & 0xFFFF).astype(f32) * dec
            for e in range(EXPS):
                wv = gains[n, e]
                half = halves[e]
                filtered = filt[n * EXPS + e, rows, :]
                mask = masks[n * EXPS + e, rows, :]
                mean = flux / jnp.maximum(weight, weight_floor)
                clipped = jnp.clip(filtered, mean - half, mean + half)
                chosen = jnp.where((mask & bit) != 0, clipped, filtered)
                flux = flux + wv * chosen
                weight = weight + wv
            if final:
                of[p, rows, :] = flux
                ow[p, rows, :] = weight
                return peak
            fbuf[rows, :] = flux
            wbuf[rows, :] = weight
            size = jnp.abs(flux)
            return jnp.maximum(peak, jnp.maximum(size[:8], size[8:]))

        peak = lax.fori_loop(0, ROWS // STEP, step, jnp.zeros((8, COLS), f32))
        if final:
            return
        for k in (4, 2, 1):
            peak = jnp.maximum(peak, pltpu.roll(peak, k, 0))
        expo = jnp.ceil(4.0 * jnp.log2(jnp.maximum(peak, 1e-30)) + 0.01)
        gain = jnp.exp2(expo * -0.25) * 32766.0
        enc = 65535.0 / jnp.full((8, COLS), top(n), f32)
        base = jnp.where(p < 4, 56, 0)

        def pack(i, c):
            rows = pl.ds(pl.multiple_of(i * 8, 8), 8)
            q = jnp.round(fbuf[rows, :] * gain).astype(i32)
            w = (wbuf[rows, :] * enc + 0.5).astype(i32)
            both = (q << 16) | w
            sb[n, p, rows, :] = both
            rext[n, p, pl.ds(pl.multiple_of(base + i * 8, 8), 8), :] = both
            return c

        lax.fori_loop(0, ROWS // 8, pack, 0)
        sb[n, p, pl.ds(pl.multiple_of(jnp.where(p < 4, 8, 48), 8), 8), :] = expo.astype(i32)
        rows_go(n, p, "start")

    def shift_rows(n, p):
        rows_go(n, p, "wait_recv")
        row_off = offs[n, p, 0]
        start = jnp.where(p < 4, 8 + MR - row_off, -row_off)
        lanes = pl.ds(pl.multiple_of(jnp.where(p % 2 == 0, MC, 0), 128), COLS)
        x = rext[n, p]
        x = jnp.concatenate([jnp.where(bits(start, 32, (88, COLS)), x[32:], x[:88]), x[88:96]], axis=0)
        x = jnp.where(bits(start, 16, (80, COLS)), x[16:], x[:80])
        x = jnp.where(bits(start, 8, (72, COLS)), x[8:], x[:72])
        moved = pltpu.roll(x, (72 - (start & 7)) % 72, 0)[:ROWS]
        own = sb[n, p, pl.ds(pl.multiple_of(jnp.where(p < 4, 8, 48), 8), 8), :]
        far = rext[n, p, pl.ds(pl.multiple_of(jnp.where(p < 4, 0, 112), 8), 8), :]
        cext[n, p, 0:ROWS, lanes] = moved
        cext[n, p, ROWS:, lanes] = jnp.where(lax.broadcasted_iota(i32, (8, COLS), 0) < 4, own, far)
        cols_go(n, p, "start")

    def plane_at(i):
        p = ORDER[0]
        for k in range(1, PLANES):
            p = jnp.where(i == k, ORDER[k], p)
        return p

    halo_go(row_halo, 0, ("up", "down"), "wait_recv")
    col_halo_send(0)
    for n in range(2, NIGHTS):
        halo_go(row_halo, n, ("up", "down"), "start")
    halo_go(col_halo, 0, ("left", "right"), "wait_recv")
    conv_range(0, 0, EXPS)
    for c in copies[1:]:
        c.wait()
    for n in range(1, NIGHTS):
        halo_go(row_halo, n, ("up", "down"), "wait_recv")
        col_halo_send(n)

    for n in range(NIGHTS):
        if n + 1 < NIGHTS:
            def body(i, c):
                p = plane_at(i)
                if n > 0:
                    cols_go(n - 1, p, "wait_recv")
                accumulate(n, p)

                @pl.when(i >= 1)
                def _():
                    relay(n, plane_at(i - 1), "start")

                @pl.when(i >= LAG)
                def _():
                    shift_rows(n, plane_at(i - LAG))
                    conv(n + 1, i - LAG)

                return c

            halo_go(col_halo, n + 1, ("left", "right"), "wait_recv")
            lax.fori_loop(0, PLANES, body, 0)

            relay(n, jnp.int32(ORDER[-1]), "start")

            def tail(i, c):
                shift_rows(n, plane_at(i))
                conv(n + 1, i)
                return c

            lax.fori_loop(PLANES - LAG, PLANES, tail, 0)
        else:
            def out_copies(p):
                return (
                    pltpu.make_async_copy(of.at[p], oflux_hbm.at[p], out_sem.at[0, p]),
                    pltpu.make_async_copy(ow.at[p], oweight_hbm.at[p], out_sem.at[1, p]),
                )

            def last(i, c):
                p = plane_at(i)
                cols_go(n - 1, p, "wait_recv")
                accumulate(n, p)
                for d in out_copies(p):
                    d.start()
                return c

            lax.fori_loop(0, PLANES, last, 0)

    def finish(p, c):
        for d in out_copies(p):
            d.wait()
        for n in range(NIGHTS - 1):
            rows_go(n, p, "wait_send")
            cols_go(n, p, "wait_send")
            relay(n, p, "wait_send")
        return c

    lax.fori_loop(0, PLANES, finish, 0)
    for n in range(NIGHTS):
        halo_go(row_halo, n, ("up", "down"), "wait_send")
        halo_go(col_halo, n, ("left", "right"), "wait_send")


def whole_call(gains, offsets, e, kv, masks, flux, weight):
    anywhere = pl.BlockSpec(memory_space=pl.ANY)
    smem = pl.BlockSpec(memory_space=pltpu.SMEM)
    dma = pltpu.SemaphoreType.DMA
    n = NIGHTS - 1
    vm = pltpu.VMEM
    return pl.pallas_call(
        whole_kernel,
        in_specs=[smem, smem, anywhere, pl.BlockSpec(memory_space=pltpu.VMEM), anywhere, anywhere, anywhere],
        out_specs=[anywhere, anywhere],
        out_shape=[jax.ShapeDtypeStruct((PLANES, ROWS, COLS), f32)] * 2,
        scratch_shapes=[
            vm((NEXP, 96, COLS), bf16),
            vm((NEXP, ROWS, COLS), i32),
            vm((PLANES, ROWS, COLS), f32),
            vm((PLANES, ROWS, COLS), f32),
            vm((NEXP, ROWS, COLS), f32),
            vm((256, 768), bf16),
            vm((768, 640), bf16),
            vm((NIGHTS, 2, 96, 128), bf16),
            vm((NIGHTS, 2, 96, 128), bf16),
            vm((ROWS, COLS), f32),
            vm((ROWS, COLS), f32),
            vm((n, PLANES, ROWS, COLS), i32),
            vm((n, PLANES, 120, COLS), i32),
            vm((n, PLANES, 72, 1024), i32),
            vm((n, 2, 56, COLS), i32),
            vm((PLANES, ROWS, COLS), f32),
            vm((PLANES, ROWS, COLS), f32),
            dma((4,)), dma((2, PLANES)),
            dma((NIGHTS, 2)), dma((NIGHTS, 2)), dma((NIGHTS, 2)), dma((NIGHTS, 2)),
            dma((n, PLANES)), dma((n, PLANES)), dma((n, PLANES)), dma((n, PLANES)), dma((n, 2)), dma((n, 2)),
        ],
        compiler_params=pltpu.CompilerParams(collective_id=0, has_side_effects=True, vmem_limit_bytes=60 << 20),
        name="stack",
    )(gains, offsets, e, kv, masks, flux, weight)


def kernel_rows(psf_kernels):
    lane = lax.broadcasted_iota(i32, (KS, 128), 1)
    tap = lax.broadcasted_iota(i32, (KS, 128), 0)
    place = ((lane + RAD) % 128 == tap).astype(bf16)
    k = jnp.einsum("neab,al->nebl", psf_kernels, place, preferred_element_type=f32)
    return k.reshape(NEXP, KS, 128)


def per_device(exposures, psf_kernels, clip_masks, exposure_weights, plane_offsets, flux, weight):
    e = exposures.reshape(NEXP, ROWS, COLS)
    masks = clip_masks.reshape(NEXP, ROWS, COLS)
    return tuple(whole_call(exposure_weights, plane_offsets, e, kernel_rows(psf_kernels), masks, flux, weight))


def solution(mesh):
    return jax.shard_map(
        per_device,
        mesh=mesh,
        in_specs=(
            P(None, None, "sy", "sx"),
            P(),
            P(None, None, "sy", "sx"),
            P(),
            P(),
            P(None, "sy", "sx"),
            P(None, "sy", "sx"),
        ),
        out_specs=(P(None, "sy", "sx"), P(None, "sy", "sx")),
        check_vma=False,
    )
```
